32 devices in a mesh: pair: 4 (over y, x), mat: 8 (over z, core).
Axes of the slice: x: 2, y: 2, z: 4, core: 2. Of those that a mesh axis runs over, the one named last changes fastest.
Arguments:
- operators: bfloat16 [16, 2048, 2048], P('pair', 'mat'), may hold values from -6 to 6
- left_rot: bfloat16 [2048, 2048], P('mat'), may hold values from -0.125 to 0.125
- right_rot: bfloat16 [2048, 2048], P('mat'), may hold values from -0.125 to 0.125
- integrals: float32 [1024, 1024], replicated, may hold values from -1.5 to 1.5
- pair_index: int32 [16], replicated, may hold values from 0 to 1023
- target_index: int32 [16], replicated, may hold values from 0 to 1023
Outputs:
- complement: bfloat16 [16, 2048, 2048], P('pair', None, 'mat')
The draws below stay inside these ranges and needn't reach their ends.
All inputs are finite; a program needn't handle non-finite values.
Results may differ from the reference program's by a relative error of at most 0.0063.
Values may be sent and summed in bfloat16 or wider, within the bound.
A program may use at most 192 MiB of HBM per device.

```python
import jax
import jax.numpy as jnp
from jax import lax

M = 2048
NPQ = 1024
NSEL = 16
NTGT = 16


def set_ends(values, key, least, high):
    shape = values.shape
    spot = [jax.random.randint(jax.random.fold_in(key, axis), (), 0, shape[axis]) for axis in range(len(shape))]
    values = values.at[tuple(spot)].set(least)
    longest = shape.index(max(shape))
    spot[longest] = (spot[longest] + 1) % shape[longest]
    return values.at[tuple(spot)].set(high)


def shard_levels(stream_key, dims, shards, least, high):
    gain = 1.0
    for position, shards_of in shards:
        heights = jax.random.uniform(jax.random.fold_in(jax.random.fold_in(stream_key, 6), position), (shards_of,), jnp.float32, least / len(shards), high / len(shards))
        gain = gain * jnp.repeat(jnp.exp(heights), dims[position] // shards_of).reshape((-1,) + (1,) * (len(dims) - 1 - position))
    return gain


def centred(rng, shape, width, limit, pieces=(), held_as=jnp.bfloat16):
    result = width * jax.random.normal(rng, shape, jnp.float32)
    if pieces:
        result = result * shard_levels(rng, shape, pieces, -0.22, 0.18)
    return jnp.clip(result, -limit, limit).astype(held_as)


def setup_inputs(seed: int = 0) -> dict:
    keys = jax.random.split(jax.random.key(seed), 7)
    operators = centred(keys[0], (NSEL, M, M), 1.0, 6.0, ((0, 4), (1, 8)))
    left_rot = centred(keys[1], (M, M), M ** -0.5, 0.125, ((0, 8),))
    right_rot = centred(keys[2], (M, M), M ** -0.5, 0.125, ((0, 8),))
    integrals = centred(keys[3], (NPQ, NPQ), (NSEL ** -0.5), 1.5, (), jnp.float32)
    pair_index = set_ends(jax.random.randint(keys[4], (NSEL,), 0, NPQ), jax.random.fold_in(keys[4], 1), 0, NPQ - 1).astype(jnp.int32)
    target_index = set_ends(jax.random.randint(keys[5], (NTGT,), 0, NPQ), jax.random.fold_in(keys[5], 1), 0, NPQ - 1).astype(jnp.int32)
    return dict(operators=operators, left_rot=left_rot, right_rot=right_rot, integrals=integrals, pair_index=pair_index, target_index=target_index)


def rotate_one(single, left_rot, right_rot):
    half_rot = jnp.dot(single, right_rot, preferred_element_type=jnp.float32).astype(jnp.bfloat16)
    return jnp.dot(left_rot.T, half_rot, preferred_element_type=jnp.float32).astype(jnp.bfloat16)


def reference(operators, left_rot, right_rot, integrals, pair_index, target_index):
    rotated = lax.map(lambda single: rotate_one(single, left_rot, right_rot), operators)
    coupling = integrals[target_index.astype(jnp.int32)][:, pair_index.astype(jnp.int32)].astype(jnp.bfloat16)
    weights = coupling.astype(jnp.float32)

    def assemble(row_weights):
        return jnp.einsum("k,kmn->mn", row_weights, rotated.astype(jnp.float32)).astype(jnp.bfloat16)

    return lax.map(assemble, weights)
```

```python
import jax
import jax.numpy as jnp
from jax import lax
from jax.sharding import PartitionSpec as P


def selector(indices, count):
    return (indices[:, None] == jnp.arange(count, dtype=jnp.int32)[None, :]).astype(jnp.float32)


def shards(operators, left_rot, right_rot, integrals, pair_index, target_index):
    npairs = integrals.shape[0]
    rowsel = jnp.dot(selector(target_index, npairs), integrals, precision=lax.Precision.HIGHEST)
    coupling = jnp.dot(
        rowsel, selector(pair_index, npairs).T, precision=lax.Precision.HIGHEST
    ).astype(jnp.bfloat16)
    right = lax.all_gather(right_rot, "mat", axis=0, tiled=True)
    left = lax.all_gather(left_rot, "mat", axis=0, tiled=True)
    strips = lax.all_to_all(operators, "pair", split_axis=1, concat_axis=0, tiled=True)
    mixed = jnp.einsum(
        "tk,krj->trj", coupling, strips, preferred_element_type=jnp.float32
    ).astype(jnp.bfloat16)
    half = jnp.einsum(
        "trj,jm->trm", mixed, right, preferred_element_type=jnp.float32
    ).astype(jnp.bfloat16)
    ntgt, rows, cols = half.shape
    npair = lax.axis_size("pair")
    nmat = lax.axis_size("mat")
    blocks = half.reshape(npair, ntgt // npair, rows, nmat, cols // nmat)
    blocks = blocks.transpose(0, 3, 1, 2, 4)
    blocks = blocks.reshape((npair * nmat,) + blocks.shape[2:])
    got = lax.all_to_all(blocks, ("pair", "mat"), split_axis=0, concat_axis=0, tiled=True)
    got = got.reshape((npair, nmat) + got.shape[1:])
    columns = got.transpose(2, 1, 0, 3, 4).reshape(ntgt // npair, cols, cols // nmat)
    return jnp.einsum(
        "rm,trc->tmc", left, columns, preferred_element_type=jnp.float32
    ).astype(jnp.bfloat16)


def solution(mesh):
    in_specs = (P("pair", "mat", None), P("mat", None), P("mat", None), P(), P(), P())
    out_specs = P("pair", None, "mat")
    return jax.shard_map(shards, mesh=mesh, in_specs=in_specs, out_specs=out_specs, check_vma=False)
```

```python
import jax
import jax.numpy as jnp
from jax import lax
from jax.sharding import Mesh, PartitionSpec as P


CORES = 2
MAT = ("line", "core")


def selector(indices, count):
    return (indices[:, None] == jnp.arange(count, dtype=jnp.int32)[None, :]).astype(jnp.float32)


def own_piece(mine):
    piece = mine.shape[0] // lax.axis_size("pair")
    return lax.dynamic_slice_in_dim(mine, lax.axis_index("pair") * piece, piece, 0)


def in_plane(along):
    whole = lax.all_gather(along, ("core", "pair"), axis=1)
    return whole.reshape(-1, along.shape[-1])


def shards(operators, left_rot, right_rot, integrals, pair_index, target_index):
    npairs = integrals.shape[0]
    npair = lax.axis_size("pair")
    nmat = lax.axis_size("line") * lax.axis_size("core")
    own, rows, cols = operators.shape
    piece = rows // npair
    width = cols // nmat

    right_a = right_rot
    outgoing = operators.reshape(own, npair, piece, cols).transpose(1, 0, 2, 3)
    outgoing = outgoing.reshape(npair, own * piece, cols)
    strips = lax.all_to_all(outgoing, "pair", split_axis=0, concat_axis=0, tiled=True)
    whole_a = lax.all_gather(right_a, MAT, axis=0, tiled=True)
    along_l = lax.all_gather(own_piece(left_rot), "line", axis=0)
    left = in_plane(along_l)

    rowsel = jnp.dot(selector(target_index, npairs), integrals, precision=lax.Precision.HIGHEST)
    coupling = jnp.dot(rowsel, selector(pair_index, npairs).T, precision=lax.Precision.HIGHEST).astype(jnp.bfloat16)
    strips = strips.reshape(own * npair, piece, cols)
    mixed = jnp.einsum(
        "tk,krj->trj", coupling, strips, preferred_element_type=jnp.float32
    ).astype(jnp.bfloat16)
    ntgt = mixed.shape[0]

    def half_swap(right):
        half = jnp.einsum(
            "trj,jm->trm", mixed, right, preferred_element_type=jnp.float32
        ).astype(jnp.bfloat16)
        blocks = half.reshape(npair, ntgt // npair, piece, nmat, width)
        blocks = blocks.transpose(0, 3, 1, 2, 4)
        blocks = blocks.reshape(npair * nmat, ntgt // npair * piece, width)
        return lax.all_to_all(blocks, ("pair",) + MAT, split_axis=0, concat_axis=0, tiled=True)

    def finish(got):
        got = got.reshape(npair, nmat, ntgt // npair, piece, width)
        columns = got.transpose(2, 1, 0, 3, 4).reshape(ntgt // npair, cols, width)
        return jnp.einsum(
            "rm,trc->tmc", left, columns, preferred_element_type=jnp.float32
        ).astype(jnp.bfloat16)

    got_a = half_swap(whole_a)
    return finish(got_a)


def solution(mesh):
    npair, nmat = mesh.shape["pair"], mesh.shape["mat"]
    fine = Mesh(mesh.devices.reshape(npair, nmat // CORES, CORES), ("pair",) + MAT)
    in_specs = (P("pair", MAT, None), P(MAT, None), P(MAT, None), P(), P(), P())
    out_specs = P("pair", None, MAT)
    return jax.shard_map(shards, mesh=fine, in_specs=in_specs, out_specs=out_specs, check_vma=False)
```
